32 devices in a mesh: dp: 8 (over z, y), tensor: 4 (over x, core).
Axes of the slice: x: 2, y: 2, z: 4, core: 2. Of those that a mesh axis runs over, the one named last changes fastest.
Arguments:
- hidden_in: bfloat16 [2048, 8, 768], P('tensor', 'dp'), may hold values from -6 to 6
- out_grad: bfloat16 [2048, 8, 768], P('tensor', 'dp'), may hold values from -6 to 6
- teacher: bfloat16 [1024, 8, 768], P(None, 'dp'), may hold values from -6 to 6
- valid_mask: int32 [1024, 8], P(None, 'dp'), may hold values from 0 to 1, as said below
- prefix: int32 [8], P('dp'), may hold values from 0 to 1024, as said below
- gain_attn: float32 [768], replicated, may hold values from 0.25 to 1.75
- w_qkv: bfloat16 [768, 3, 768], P(None, None, 'tensor'), may hold values from -0.21875 to 0.21875
- w_out: bfloat16 [768, 768], P('tensor'), may hold values from -3 to 3
- gain_mlp: float32 [768], replicated, may hold values from 0.25 to 1.75
- w_up: bfloat16 [768, 3072], P(None, 'tensor'), may hold values from -0.21875 to 0.21875
- b_up: bfloat16 [3072], P('tensor'), may hold values from -3 to 3
- w_down: bfloat16 [3072, 768], P('tensor'), may hold values from -0.109375 to 0.109375
- b_down: bfloat16 [768], replicated, may hold values from -3 to 3
Outputs:
- layer_out: bfloat16 [2048, 8, 768], P('tensor', 'dp')
- grad_input: float32 [2048, 8, 768], P('tensor', 'dp')
- distill_loss: float32 [], replicated
- grad_gain_attn: float32 [768], replicated
- grad_w_qkv: float32 [768, 3, 768], P(None, None, 'tensor')
- grad_w_out: float32 [768, 768], P('tensor')
- grad_gain_mlp: float32 [768], replicated
- grad_w_up: float32 [768, 3072], P(None, 'tensor')
- grad_b_up: float32 [3072], P('tensor')
- grad_w_down: float32 [3072, 768], P('tensor')
- grad_b_down: float32 [768], replicated
The draws below stay inside these ranges and needn't reach their ends.
Inputs may be any that keep to these rules, and one draw needn't show every extreme that they name: Every sequence has one or more tokens with valid_mask 1. Some sequence has prefix 1024 and some prefix 0.
All inputs are finite; a program needn't handle non-finite values.
Results may differ from the reference program's by a relative error of at most 0.012.
The reference program's roundings to bfloat16 on the way count: a program that leaves them out, or rounds other values in their place, can miss the bound.
Values may be sent and summed in bfloat16 or wider, within the bound.
No kernel may reach another device: no remote copies, remote signals or barrier semaphores. Data moves between devices by JAX's collectives and lax.ppermute only.
A program may use at most 192 MiB of HBM per device.

```python
import jax
import jax.numpy as jnp
from jax import lax

D = 768
HEADS = 12
HEAD_DIM = 64
FF = 3072
BLOCK = 16
L = 1024
ROWS = 2048
SEQS = 8
TOKENS = 8192


def draw_valid_mask(key, part):
    key_level, key_pick = jax.random.split(key)
    levels = jax.random.randint(key_level, (L, SEQS), 0, 1024)
    seq_index = jnp.arange(SEQS, dtype=jnp.int32)
    threshold = 256 + 512 * seq_index // max(SEQS - 1, 1)
    chosen = jax.random.randint(key_pick, (SEQS,), 0, L)
    forced = jnp.arange(L, dtype=jnp.int32)[:, None] == chosen[None, :]
    return ((levels < threshold[None, :]) | forced).astype(jnp.int32)


def draw_prefix(key, part):
    key_base, key_top, key_zero = jax.random.split(key, 3)
    prefix_len = jax.random.randint(key_base, (SEQS,), 0, L + 1)
    top_index = jax.random.randint(key_top, (), 0, SEQS)
    zero_index = (top_index + 1 + jax.random.randint(key_zero, (), 0, max(SEQS - 1, 1))) % SEQS
    positions = jnp.arange(SEQS, dtype=jnp.int32)
    prefix_len = jnp.where(positions == top_index, L, prefix_len)
    prefix_len = jnp.where(positions == zero_index, 0, prefix_len)
    return prefix_len.astype(jnp.int32)


def steps_of(key, extent, cuts, low, high):
    level = 1.0
    for axis_at, blocks in cuts:
        draws = jax.random.uniform(jax.random.fold_in(jax.random.fold_in(key, 6), axis_at), (blocks,), jnp.float32, low / len(cuts), high / len(cuts))
        level = level * jnp.repeat(jnp.exp(draws), extent[axis_at] // blocks).reshape((-1,) + (1,) * (len(extent) - 1 - axis_at))
    return level


def bell_draw(rng, dims, scale, reach, pieces=(), held_as=jnp.bfloat16):
    array = jax.random.normal(rng, dims, jnp.float32) * scale
    if len(pieces) > 0:
        array = steps_of(rng, dims, pieces, -0.22, 0.18) * array
    return jnp.clip(array, min=-reach, max=reach).astype(held_as)


def setup_inputs(seed: int = 0) -> dict:
    arg_keys = jax.random.split(jax.random.key(seed), 14)
    return {
        "hidden_in": bell_draw(arg_keys[0], (ROWS, SEQS, D), 1.0, 6.0, ((0, 4), (1, 8))),
        "out_grad": bell_draw(arg_keys[1], (ROWS, SEQS, D), 1.0, 6.0, ((0, 4), (1, 8))),
        "teacher": bell_draw(arg_keys[2], (L, SEQS, D), 1.0, 6.0, ((1, 8),)),
        "valid_mask": draw_valid_mask(jax.random.fold_in(arg_keys[13], 71), 0),
        "prefix": draw_prefix(jax.random.fold_in(arg_keys[13], 71), 0),
        "gain_attn": jnp.clip(1.0 + 0.15 * jax.random.normal(arg_keys[5], (D,), jnp.float32), 0.25, 1.75),
        "w_qkv": bell_draw(arg_keys[6], (D, 3, D), D ** -0.5, 0.21875, ((2, 4),)),
        "w_out": bell_draw(arg_keys[7], (D, D), (max(1, D // 192)) ** -0.5, 3.0, ((0, 4),)),
        "gain_mlp": jnp.clip(1.0 + 0.15 * jax.random.normal(arg_keys[8], (D,), jnp.float32), 0.25, 1.75),
        "w_up": bell_draw(arg_keys[9], (D, FF), D ** -0.5, 0.21875, ((1, 4),)),
        "b_up": bell_draw(arg_keys[10], (FF,), 0.5, 3.0, ((0, 4),)),
        "w_down": bell_draw(arg_keys[11], (FF, D), FF ** -0.5, 0.109375, ((0, 4),)),
        "b_down": bell_draw(arg_keys[12], (D,), 0.5, 3.0),
    }


@jax.custom_vjp
def low(v):
    return lax.optimization_barrier(v.astype(jnp.bfloat16)).astype(jnp.float32)

@jax.custom_vjp
def low_back(v):
    return v

def low_keep(v):
    return (low(v), None)

def low_pass(kept, grad):
    return (grad,)

def back_keep(v):
    return (v, None)

def back_low(kept, grad):
    return (low(grad),)
low.defvjp(low_keep, low_pass)
low_back.defvjp(back_keep, back_low)
norm_eps = 1e-05

def layer_norm(values, gain):
    average = lax.optimization_barrier(jnp.mean(values, -1, keepdims=True))
    centred = values - average
    spread = lax.optimization_barrier(jnp.mean(centred * centred, -1, keepdims=True))
    return centred * lax.rsqrt(spread + norm_eps) * gain

def rotate(values, positions):
    half = values.shape[-1] // 2
    freqs = jnp.exp(-jnp.log(10000.0) * jnp.arange(half, dtype=jnp.float32) * 2.0 / values.shape[-1])
    angles = positions.astype(jnp.float32)[:, None] * freqs[None, :]
    shape = (values.shape[0],) + (1,) * (values.ndim - 2) + (half,)
    cosine = jnp.cos(angles).reshape(shape)
    sine = jnp.sin(angles).reshape(shape)
    former = values[..., :half]
    latter = values[..., half:]
    return jnp.concatenate([former * cosine - latter * sine, latter * cosine + former * sine], -1)

def allowed(query_rows, key_rows, length, limit):
    noisy_q = (query_rows < length)[:, None]
    noisy_k = (key_rows < length)[None, :]
    block_q = (query_rows % length // BLOCK)[:, None]
    block_k = (key_rows % length // BLOCK)[None, :]
    place_k = (key_rows % length)[None, :]
    same = noisy_q & noisy_k & (block_q == block_k)
    earlier = noisy_q & ~noisy_k & (block_k < block_q)
    clean = ~noisy_q & ~noisy_k & (block_k <= block_q)
    given = ~noisy_k & (place_k < limit)
    return same | earlier | clean | given

def one_sequence(params, row_in, limit, teach_rows, valid_rows):
    gain_one, wqkv, wout, gain_two, wup, bup, wdown, bdown = params
    row_total = row_in.shape[0]
    length = row_total // 2
    highest = lax.Precision.HIGHEST
    act_one = low(layer_norm(row_in, gain_one))
    qkv = low_back(jnp.einsum('rd,dcf->rcf', act_one, wqkv, precision=highest))
    positions = jnp.arange(row_total, dtype=jnp.int32) % length
    queries = low(rotate(qkv[:, 0].reshape(row_total, HEADS, HEAD_DIM), positions))
    keys_all = low(rotate(qkv[:, 1].reshape(row_total, HEADS, HEAD_DIM), positions))
    values = low(qkv[:, 2].reshape(row_total, HEADS, HEAD_DIM))
    scores = low_back(jnp.einsum('qhe,khe->hqk', queries, keys_all, precision=highest)) * (1.0 / HEAD_DIM ** 0.5)
    rows_idx = jnp.arange(row_total, dtype=jnp.int32)
    mask = allowed(rows_idx, rows_idx, length, limit)
    scores = jnp.where(mask[None], scores, -1e+30)
    peak = lax.optimization_barrier(jnp.max(scores, -1, keepdims=True))
    expo = jnp.exp(scores - peak)
    probs = expo / lax.optimization_barrier(jnp.sum(expo, -1, keepdims=True))
    heads_out = jnp.einsum('hqk,khe->qhe', low(probs), values, precision=highest).reshape(row_total, D)
    attn = low_back(jnp.dot(low(low_back(heads_out)), wout, precision=highest))
    resid = row_in + attn
    act_two = low(layer_norm(resid, gain_two))
    pre = low_back(jnp.dot(act_two, wup, precision=highest)) + bup
    hidden = jax.nn.gelu(pre, approximate=True)
    out_full = resid + low_back(jnp.dot(low(hidden), wdown, precision=highest)) + bdown
    diff = out_full[:length] - teach_rows
    part_sum = jnp.sum(valid_rows * lax.optimization_barrier(jnp.mean(diff * diff, -1)))
    return (out_full, part_sum)

def reference(hidden_in, out_grad, teacher, valid_mask, prefix, gain_attn, w_qkv, w_out, gain_mlp, w_up, b_up, w_down, b_down):
    seq_in = jnp.transpose(hidden_in.astype(jnp.float32), (1, 0, 2))
    teach_seq = jnp.transpose(teacher.astype(jnp.float32), (1, 0, 2))
    valid_seq = jnp.transpose(valid_mask, (1, 0)).astype(jnp.float32)
    count = jnp.sum(valid_mask).astype(jnp.float32)
    params = (gain_attn.astype(jnp.float32), w_qkv.astype(jnp.float32), w_out.astype(jnp.float32), gain_mlp.astype(jnp.float32), w_up.astype(jnp.float32), b_up.astype(jnp.float32), w_down.astype(jnp.float32), b_down.astype(jnp.float32))
    checked = jax.checkpoint(one_sequence)

    def forward(seq_values, weights):

        def step(running, item):
            row_in, limit, teach_rows, valid_rows = item
            out_rows, part_sum = checked(weights, row_in, limit, teach_rows, valid_rows)
            return (running + part_sum, out_rows)
        running, outputs = lax.scan(step, jnp.zeros((), jnp.float32), (seq_values, prefix, teach_seq, valid_seq))
        return (outputs, running / count)
    (outputs, distill_loss), pullback = jax.vjp(forward, seq_in, params)
    weight_ct = jnp.asarray(TOKENS * D / 2.0, dtype=jnp.float32)
    grad_seq, grads = pullback((jnp.transpose(out_grad.astype(jnp.float32), (1, 0, 2)), weight_ct))
    layer_out = jnp.transpose(outputs, (1, 0, 2)).astype(jnp.bfloat16)
    grad_input = jnp.transpose(grad_seq, (1, 0, 2))
    return (layer_out, grad_input, distill_loss, grads[0], grads[1], grads[2], grads[3], grads[4], grads[5], grads[6], grads[7])
```

```python
import functools
import math

import jax
import jax.numpy as jnp
from jax import lax
from jax.experimental import pallas as pl
from jax.experimental.pallas import tpu as pltpu
from jax.sharding import PartitionSpec as P

HEAD_DIM = 64
BLOCK = 16
NEG = -1e30
norm_eps = 1e-05
SCALE = 1.0 / math.sqrt(HEAD_DIM)
LOW = jnp.bfloat16
WIDE = jnp.float32
VMEM = pl.BlockSpec(memory_space=pltpu.VMEM)
SMEM = pl.BlockSpec(memory_space=pltpu.SMEM)
PARAMS = pltpu.CompilerParams(vmem_limit_bytes=58 << 20)


def dot_nn(a, b):
    return lax.dot_general(a, b, (((1,), (0,)), ((), ())), preferred_element_type=WIDE)


def dot_nt(a, b):
    return lax.dot_general(a, b, (((1,), (1,)), ((), ())), preferred_element_type=WIDE)


def dot_tn(a, b):
    return lax.dot_general(a, b, (((0,), (0,)), ((), ())), preferred_element_type=WIDE)


def normalize(x):
    average = jnp.mean(x, -1, keepdims=True)
    centred = x - average
    spread = jnp.mean(centred * centred, -1, keepdims=True)
    inverse = lax.rsqrt(spread + norm_eps)
    return centred * inverse, inverse


def norm_input_grad(grad, gain, hat, inverse):
    scaled = grad * gain
    first = jnp.mean(scaled, -1, keepdims=True)
    second = jnp.mean(scaled * hat, -1, keepdims=True)
    return inverse * (scaled - first - hat * second)


def head_lanes(rows, width, h):
    lane = lax.broadcasted_iota(jnp.int32, (rows, width), 1)
    return (lane >= h * HEAD_DIM) & (lane < (h + 1) * HEAD_DIM)


def rope_matrix(width):
    half = HEAD_DIM // 2
    r = lax.broadcasted_iota(jnp.int32, (width, width), 0)
    c = lax.broadcasted_iota(jnp.int32, (width, width), 1)
    first = (c % HEAD_DIM) < half
    minus = jnp.where(first & (r == c + half), -1.0, 0.0)
    plus = jnp.where((~first) & (r + half == c), 1.0, 0.0)
    return (minus + plus).astype(LOW)


def attn_forward_body(
    meta_ref, x0, x1, x2, x3, gain_ref, w_ref, cos_ref, sin_ref,
    act_ref, q_ref, k_ref, v_ref, mix_ref, lse_ref,
    wr_s, kh_s, vh_s, *, tile,
):
    rows, width = q_ref.shape
    own = x0.shape[0]
    length = rows // 2
    heads = width // HEAD_DIM
    per = length // tile
    prefix = meta_ref[0]
    me = meta_ref[1]
    rmat = rope_matrix(width)
    wr_s[0] = dot_nn(w_ref[0], rmat).astype(LOW)
    wr_s[1] = dot_nn(w_ref[1], rmat).astype(LOW)
    for rel, x_ref in enumerate((x0, x1, x2, x3)):
        base = (me ^ rel) * own

        def project(i, carry):
            here = pl.ds(pl.multiple_of(i * tile, tile), tile)
            start = base + i * tile
            at = pl.ds(pl.multiple_of(start, tile), tile)
            pos = pl.ds(pl.multiple_of(lax.rem(start, length), tile), tile)
            hat, _ = normalize(x_ref[here, :].astype(WIDE))
            act = (hat * gain_ref[...]).astype(LOW)
            act_ref[rel, here, :] = act
            c = cos_ref[pos, :]
            s = sin_ref[pos, :]
            q = dot_nn(act, w_ref[0]) * c + dot_nn(act, wr_s[0]) * s
            q_ref[at, :] = (q.astype(LOW).astype(WIDE) * SCALE).astype(LOW)
            k = (dot_nn(act, w_ref[1]) * c + dot_nn(act, wr_s[1]) * s).astype(LOW)
            v = dot_nn(act, w_ref[2]).astype(LOW)
            k_ref[at, :] = k
            v_ref[at, :] = v
            zero = jnp.zeros_like(k)
            for h in range(heads):
                lanes = head_lanes(tile, width, h)
                kh_s[h, at, :] = jnp.where(lanes, k, zero)
                vh_s[h, at, :] = jnp.where(lanes, v, zero)
            return carry

        lax.fori_loop(0, own // tile, project, 0)

    def attend(i, noisy):
        start = pl.multiple_of(i * tile + (0 if noisy else length), tile)
        at = pl.ds(start, tile)
        q = q_ref[at, :]
        row = i * tile + lax.broadcasted_iota(jnp.int32, (tile, 1), 0)
        limit = jnp.maximum(prefix, row // BLOCK * BLOCK + (0 if noisy else BLOCK))
        col = lax.broadcasted_iota(jnp.int32, (tile, length), 1)
        lane = lax.broadcasted_iota(jnp.int32, (tile, 128), 1)
        out = jnp.zeros((tile, width), WIDE)
        lse = jnp.zeros((tile, 128), WIDE)
        if noisy:
            qi = lax.broadcasted_iota(jnp.int32, (tile, tile), 0) // BLOCK
            ki = lax.broadcasted_iota(jnp.int32, (tile, tile), 1) // BLOCK
        for h in range(heads):
            s = dot_nt(q, kh_s[h, length:, :])
            s = jnp.where(col < limit, s, NEG)
            peak = jnp.max(s, -1, keepdims=True)
            if noisy:
                d = dot_nt(q, kh_s[h, at, :])
                d = jnp.where(qi == ki, d, NEG)
                peak = jnp.maximum(peak, jnp.max(d, -1, keepdims=True))
            e = jnp.exp(s - peak)
            total = jnp.sum(e, -1, keepdims=True)
            o = dot_nn(e.astype(LOW), vh_s[h, length:, :])
            if noisy:
                f = jnp.exp(d - peak)
                total = total + jnp.sum(f, -1, keepdims=True)
                o = o + dot_nn(f.astype(LOW), vh_s[h, at, :])
            out = out + o * (1.0 / total)
            lse = jnp.where(lane == h, peak + jnp.log(total), lse)
        owner = lax.div(start, own)
        inner = pl.ds(pl.multiple_of(start - owner * own, tile), tile)
        mix_ref[owner ^ me, inner, :] = out.astype(LOW)
        lse_ref[at, :] = lse

    def noisy_step(i, carry):
        attend(i, True)
        return carry

    def clean_step(i, carry):
        attend(i, False)
        return carry

    lax.fori_loop(0, per, noisy_step, 0)
    lax.fori_loop(0, per, clean_step, 0)


def attn_forward(meta, pieces, gain, w3, cos, sin, tile):
    own, d = pieces[0].shape
    rows = own * len(pieces)
    width = w3.shape[2]
    heads = width // HEAD_DIM
    sds = jax.ShapeDtypeStruct
    return pl.pallas_call(
        functools.partial(attn_forward_body, tile=tile),
        out_shape=(
            sds((len(pieces), own, d), LOW),
            sds((rows, width), LOW),
            sds((rows, width), LOW),
            sds((rows, width), LOW),
            sds((len(pieces), own, width), LOW),
            sds((rows, 128), WIDE),
        ),
        in_specs=[SMEM] + [VMEM] * 8,
        out_specs=(VMEM,) * 6,
        scratch_shapes=[
            pltpu.VMEM((2, d, width), LOW),
            pltpu.VMEM((heads, rows, width), LOW),
            pltpu.VMEM((heads, rows, width), LOW),
        ],
        compiler_params=PARAMS,
        name="attn_forward",
    )(meta, *pieces, gain, w3, cos, sin)


def attn_backward_body(
    meta_ref, q_ref, k_ref, v_ref, o_ref, d0, d1, d2, d3, lse_ref, cos_ref, sin_ref,
    g_ref,
    do_s, kh_s, vh_s, qh_s, dh_s, kt_s, delta_s, dk_s, dv_s, dq_s, *, tile,
):
    rows, width = q_ref.shape
    length = rows // 2
    heads = width // HEAD_DIM
    per = length // tile
    own = d0.shape[0]
    prefix = meta_ref[0]
    me = meta_ref[1]
    hrow = lax.broadcasted_iota(jnp.int32, (8, width), 0)
    hlane = lax.broadcasted_iota(jnp.int32, (8, width), 1)
    pick = jnp.where(hlane // HEAD_DIM == hrow, 1.0, 0.0).astype(LOW)
    for rel, d_ref in enumerate((d0, d1, d2, d3)):
        base = (me ^ rel) * own

        def prepare(i, carry):
            here = pl.ds(pl.multiple_of(i * tile, tile), tile)
            start = pl.multiple_of(base + i * tile, tile)
            t = lax.div(start, tile)
            at = pl.ds(start, tile)
            q = q_ref[at, :]
            k = k_ref[at, :]
            v = v_ref[at, :]
            do = d_ref[here, :]
            do_s[at, :] = do
            zero = jnp.zeros_like(q)
            for h in range(heads):
                lanes = head_lanes(tile, width, h)
                qh_s[t, h * tile : (h + 1) * tile, :] = jnp.where(lanes, q, zero)
                dh_s[t, h * tile : (h + 1) * tile, :] = jnp.where(lanes, do, zero)
                kh_s[h, at, :] = jnp.where(lanes, k, zero)
                vh_s[h, at, :] = jnp.where(lanes, v, zero)
            kt_s[t] = k.T
            prod = do.astype(WIDE) * o_ref[rel, here, :].astype(WIDE)
            high = prod.astype(LOW)
            rest = (prod - high.astype(WIDE)).astype(LOW)
            delta_s[t] = dot_nt(pick, high) + dot_nt(pick, rest)
            return carry

        lax.fori_loop(0, own // tile, prepare, 0)
    dk_s[...] = jnp.zeros_like(dk_s)
    dv_s[...] = jnp.zeros_like(dv_s)

    def step(i, noisy):
        t = i if noisy else i + per
        at = pl.ds(pl.multiple_of(t * tile, tile), tile)
        q = q_ref[at, :]
        do = do_s[at, :]
        qh = qh_s[t]
        dh = dh_s[t]
        col = i * tile + lax.broadcasted_iota(jnp.int32, (1, tile), 1)
        limit = jnp.maximum(prefix, col // BLOCK * BLOCK + (0 if noisy else BLOCK))
        key = lax.broadcasted_iota(jnp.int32, (length, tile), 0)
        if noisy:
            ki = lax.broadcasted_iota(jnp.int32, (tile, tile), 0) // BLOCK
            qi = lax.broadcasted_iota(jnp.int32, (tile, tile), 1) // BLOCK
        ps, dss, pd, dd, dqs = [], [], [], [], []
        for h in range(heads):
            lanes = slice(h * HEAD_DIM, (h + 1) * HEAD_DIM)
            lse = lse_ref[t, h : h + 1, :]
            delta = delta_s[t, h : h + 1, :]
            s = dot_nt(kh_s[h, length:, :], q)
            p = jnp.exp(jnp.where(key < limit, s, NEG) - lse)
            dp = dot_nt(vh_s[h, length:, :], do)
            ds = (p * (dp - delta)).astype(LOW)
            ps.append(p.astype(LOW))
            dss.append(ds)
            dq = jnp.zeros((HEAD_DIM, tile), WIDE)
            for j in range(per):
                dq = dq + dot_nn(kt_s[per + j, lanes, :], ds[j * tile : (j + 1) * tile, :])
            if noisy:
                s = dot_nt(kh_s[h, at, :], q)
                p = jnp.exp(jnp.where(ki == qi, s, NEG) - lse)
                dp = dot_nt(vh_s[h, at, :], do)
                ds = (p * (dp - delta)).astype(LOW)
                pd.append(p.astype(LOW))
                dd.append(ds)
                dq = dq + dot_nn(kt_s[t, lanes, :], ds)
            dqs.append(dq)
        dk_s[length:, :] += dot_nn(jnp.concatenate(dss, 1), qh)
        dv_s[length:, :] += dot_nn(jnp.concatenate(ps, 1), dh)
        if noisy:
            dk_s[at, :] = dot_nn(jnp.concatenate(dd, 1), qh)
            dv_s[at, :] = dot_nn(jnp.concatenate(pd, 1), dh)
        dq_s[at, :] = jnp.concatenate(dqs, 0).T * SCALE

    def noisy_step(i, carry):
        step(i, True)
        return carry

    def clean_step(i, carry):
        step(i, False)
        return carry

    lax.fori_loop(0, per, noisy_step, 0)
    lax.fori_loop(0, per, clean_step, 0)
    rmat = rope_matrix(width)

    def unrotate(g, c, s):
        high = g.astype(LOW)
        rest = (g - high.astype(WIDE)).astype(LOW)
        return (g * c - (dot_nn(high, rmat) + dot_nn(rest, rmat)) * s).astype(LOW)

    def finish(i, carry):
        start = pl.multiple_of(i * tile, tile)
        at = pl.ds(start, tile)
        pos = pl.ds(pl.multiple_of(lax.rem(start, length), tile), tile)
        owner = lax.div(start, own)
        inner = pl.ds(pl.multiple_of(start - owner * own, tile), tile)
        rel = owner ^ me
        c = cos_ref[pos, :]
        s = sin_ref[pos, :]
        g_ref[0, rel, inner, :] = unrotate(dq_s[at, :], c, s)
        g_ref[1, rel, inner, :] = unrotate(dk_s[at, :], c, s)
        g_ref[2, rel, inner, :] = dv_s[at, :].astype(LOW)
        return carry

    lax.fori_loop(0, 2 * per, finish, 0)


def attn_backward(meta, q, k, v, mix, grads, lse, cos, sin, tile):
    rows, width = q.shape
    heads = width // HEAD_DIM
    own = grads[0].shape[0]
    n = rows // tile
    lse_t = jnp.transpose(lse[:, :8].reshape(n, tile, 8), (0, 2, 1))
    return pl.pallas_call(
        functools.partial(attn_backward_body, tile=tile),
        out_shape=jax.ShapeDtypeStruct((3, len(grads), own, width), LOW),
        in_specs=[SMEM] + [VMEM] * 11,
        out_specs=VMEM,
        scratch_shapes=[
            pltpu.VMEM((rows, width), LOW),
            pltpu.VMEM((heads, rows, width), LOW),
            pltpu.VMEM((heads, rows, width), LOW),
            pltpu.VMEM((n, heads * tile, width), LOW),
            pltpu.VMEM((n, heads * tile, width), LOW),
            pltpu.VMEM((n, width, tile), LOW),
            pltpu.VMEM((n, 8, tile), WIDE),
            pltpu.VMEM((rows, width), WIDE),
            pltpu.VMEM((rows, width), WIDE),
            pltpu.VMEM((rows, width), WIDE),
        ],
        compiler_params=PARAMS,
        name="attn_backward",
    )(meta, q, k, v, mix, *grads, lse_t, cos, sin)


def mlp_body(
    ratio_ref, x_ref, m0, m1, m2, m3, o0, o1, o2, o3, u0, u1, u2, u3, w0, w1, w2, w3,
    b0, b1, b2, b3, gain_ref, bdown_ref, teach_ref, valid_ref, og_ref,
    out_ref, hid_ref, act_ref, gol_ref, gpl_ref, gres_ref, grl_ref,
    g0_ref, g1_ref, g2_ref, g3_ref, vec_ref,
    slope_s,
):
    resid = x_ref[...].astype(WIDE)
    for m_ref, o_ref in ((m0, o0), (m1, o1), (m2, o2), (m3, o3)):
        resid = resid + dot_nn(m_ref[...], o_ref[...])
    hat, inverse = normalize(resid)
    gain = gain_ref[...]
    act = (hat * gain).astype(LOW)
    act_ref[...] = act
    out = resid + bdown_ref[...].astype(WIDE)
    ups = (u0, u1, u2, u3)
    downs = (w0, w1, w2, w3)
    root = math.sqrt(2.0 / math.pi)
    for b, bias_ref in enumerate((b0, b1, b2, b3)):
        pre = dot_nn(act, ups[b][...]) + bias_ref[...].astype(WIDE)
        square = pre * pre
        bend = jnp.tanh(pre * (root + root * 0.044715 * square))
        half = 0.5 + 0.5 * bend
        hidden = (pre * half).astype(LOW)
        hid_ref[b] = hidden
        slope_s[b] = half + (0.5 * pre) * (1.0 - bend * bend) * (root + 3.0 * root * 0.044715 * square)
        out = out + dot_nn(hidden, downs[b][...])
    out_ref[...] = out.astype(LOW)
    diff = out - teach_ref[...].astype(WIDE)
    valid = valid_ref[...]
    loss = jnp.sum(valid * jnp.mean(diff * diff, -1, keepdims=True), 0, keepdims=True)
    grad_out = og_ref[...].astype(WIDE) + (ratio_ref[0] * valid) * diff
    gres_ref[...] = grad_out
    gol = grad_out.astype(LOW)
    gol_ref[...] = gol
    vec_ref[4:5, :] = jnp.sum(grad_out, 0, keepdims=True)
    gact = jnp.zeros(resid.shape, WIDE)
    for b in range(4):
        gpre = dot_nt(gol, downs[b][...]) * slope_s[b]
        vec_ref[b : b + 1, :] = jnp.sum(gpre, 0, keepdims=True)
        gpl = gpre.astype(LOW)
        gpl_ref[b] = gpl
        gact = gact + dot_nt(gpl, ups[b][...])
    vec_ref[5:6, :] = jnp.sum(gact * hat, 0, keepdims=True)
    vec_ref[6:7, :] = jnp.broadcast_to(loss, (1, resid.shape[1]))
    vec_ref[7:8, :] = jnp.zeros((1, resid.shape[1]), WIDE)
    gres = gres_ref[...] + norm_input_grad(gact, gain, hat, inverse)
    gres_ref[...] = gres
    grl = gres.astype(LOW)
    grl_ref[...] = grl
    for g_ref, o_ref in ((g0_ref, o0), (g1_ref, o1), (g2_ref, o2), (g3_ref, o3)):
        g_ref[...] = dot_nt(grl, o_ref[...]).astype(LOW)


def mlp(ratio, x, mixed, outs, ups, downs, biases, gain, b_down, teach, valid, out_grad):
    own, d = x.shape
    width = mixed[0].shape[1]
    ff = ups[0].shape[1]
    sds = jax.ShapeDtypeStruct
    return pl.pallas_call(
        mlp_body,
        out_shape=(
            sds((own, d), LOW),
            sds((4, own, ff), LOW),
            sds((own, d), LOW),
            sds((own, d), LOW),
            sds((4, own, ff), LOW),
            sds((own, d), WIDE),
            sds((own, d), LOW),
            sds((own, width), LOW),
            sds((own, width), LOW),
            sds((own, width), LOW),
            sds((own, width), LOW),
            sds((8, d), WIDE),
        ),
        in_specs=[SMEM] + [VMEM] * 26,
        out_specs=(VMEM,) * 12,
        scratch_shapes=[pltpu.VMEM((4, own, ff), WIDE)],
        compiler_params=PARAMS,
        name="mlp",
    )(ratio, x, *mixed, *outs, *ups, *downs, *biases, gain, b_down, teach, valid, out_grad)


def down_grad_body(hid_ref, gol_ref, send_ref, keep_ref):
    gol = gol_ref[...]
    for b in range(4):
        grad = dot_tn(hid_ref[b], gol).astype(LOW)
        if b % 2:
            send_ref[b // 2] = grad
        else:
            keep_ref[b // 2] = grad


def up_grad_body(act_ref, gpl_ref, m0, m1, m2, m3, grl_ref, send_ref, keep_ref):
    act_t = act_ref[...].T
    d = act_t.shape[0]
    grl = grl_ref[...]
    for b, m_ref in enumerate((m0, m1, m2, m3)):
        target = send_ref if b % 2 else keep_ref
        target[b // 2, :d, :] = dot_nn(act_t, gpl_ref[b]).astype(LOW)
        target[b // 2, d:, :] = dot_tn(m_ref[...], grl).astype(LOW)


def down_grad(hid, gol):
    _, own, ff = hid.shape
    shape = jax.ShapeDtypeStruct((2, ff, gol.shape[1]), LOW)
    return pl.pallas_call(
        down_grad_body,
        out_shape=(shape, shape),
        in_specs=[VMEM] * 2,
        out_specs=(VMEM,) * 2,
        compiler_params=PARAMS,
        name="down_grad",
    )(hid, gol)


def up_grad(act, gpl, mixed, grl):
    d = act.shape[1]
    width = mixed[0].shape[1]
    shape = jax.ShapeDtypeStruct((2, d + width, gpl.shape[2]), LOW)
    return pl.pallas_call(
        up_grad_body,
        out_shape=(shape, shape),
        in_specs=[VMEM] * 7,
        out_specs=(VMEM,) * 2,
        compiler_params=PARAMS,
        name="up_grad",
    )(act, gpl, *mixed, grl)


def rows_grad_body(g_ref, w_ref, send_ref, keep_ref):
    for b in range(4):
        total = dot_nt(g_ref[0, b], w_ref[0])
        total = total + dot_nt(g_ref[1, b], w_ref[1])
        total = total + dot_nt(g_ref[2, b], w_ref[2])
        if b % 2:
            send_ref[b // 2] = total.astype(LOW)
        else:
            keep_ref[b // 2] = total.astype(LOW)


def rows_grad(g, w3):
    _, _, own, width = g.shape
    shape = jax.ShapeDtypeStruct((2, own, w3.shape[1]), LOW)
    return pl.pallas_call(
        rows_grad_body,
        out_shape=(shape, shape),
        in_specs=[VMEM] * 2,
        out_specs=(VMEM,) * 2,
        compiler_params=PARAMS,
        name="rows_grad",
    )(g, w3)


def qkv_grad_body(act_ref, g_ref, w_ref, grad_ref, part_ref):
    part = None
    for c in range(3):
        grad = dot_tn(act_ref[0], g_ref[c, 0])
        for b in range(1, 4):
            grad = grad + dot_tn(act_ref[b], g_ref[c, b])
        grad_ref[c] = grad.astype(LOW)
        own = jnp.sum(grad * w_ref[c].astype(WIDE), -1, keepdims=True)
        part = own if part is None else part + own
    part_ref[...] = jnp.broadcast_to(part, part_ref.shape)


def qkv_grad(act, g, w3):
    _, d, width = w3.shape
    sds = jax.ShapeDtypeStruct
    return pl.pallas_call(
        qkv_grad_body,
        out_shape=(sds((3, d, width), LOW), sds((d, 128), WIDE)),
        in_specs=[VMEM] * 3,
        out_specs=(VMEM,) * 2,
        compiler_params=PARAMS,
        name="qkv_grad",
    )(act, g, w3)


def input_grad_body(x_ref, gain_ref, keep_ref, near_ref, far_ref, gres_ref, grad_ref):
    hat, inverse = normalize(x_ref[...].astype(WIDE))
    grad = keep_ref[0].astype(WIDE) + near_ref[0].astype(WIDE) + far_ref[...].astype(WIDE)
    grad_ref[...] = gres_ref[...] + norm_input_grad(grad, gain_ref[...], hat, inverse)


def input_grad(x, gain, keep, near, far, gres):
    return pl.pallas_call(
        input_grad_body,
        out_shape=jax.ShapeDtypeStruct(x.shape, WIDE),
        in_specs=[VMEM] * 6,
        out_specs=VMEM,
        compiler_params=PARAMS,
        name="input_grad",
    )(x, gain, keep, near, far, gres)


def swap(x, axis, mask):
    n = lax.axis_size(axis)
    return lax.ppermute(x, axis, [(i, i ^ mask) for i in range(n)])


def gather_pieces(x):
    far = swap(x, "tensor", 2)
    return (x, swap(x, "tensor", 1), far, swap(far, "tensor", 1))


def exchange(pieces):
    return (pieces[0],) + tuple(swap(pieces[b], "tensor", b) for b in range(1, 4))


def dp_stages():
    n = lax.axis_size("dp")
    bits = n.bit_length() - 1
    stages, low = [], 0
    while low < bits:
        size = 1 if low == 0 else min(2, bits - low)
        stages.append((low, size))
        low += size
    return stages


def sum_all(x):
    for low, size in dp_stages():
        x = x + sum(swap(x, "dp", m << low) for m in range(1, 1 << size))
    return x


def reduce_over_dp(x):
    me = lax.axis_index("dp")
    stages = dp_stages()
    for low, size in stages:
        count = 1 << size
        mine = (me >> low) & (count - 1)
        rows = x.shape[0] // count
        parts = x.reshape((count, rows) + x.shape[1:])
        total = lax.dynamic_index_in_dim(parts, mine, 0, False).astype(WIDE)
        for m in range(1, count):
            piece = lax.dynamic_index_in_dim(parts, mine ^ m, 0, False)
            total = total + swap(piece, "dp", m << low).astype(WIDE)
        x = total.astype(LOW)
    for low, size in reversed(stages):
        count = 1 << size
        mine = (me >> low) & (count - 1)
        whole = jnp.zeros((count,) + x.shape, LOW)
        whole = lax.dynamic_update_index_in_dim(whole, x, mine, 0)
        for m in range(1, count):
            whole = lax.dynamic_update_index_in_dim(whole, swap(x, "dp", m << low), mine ^ m, 0)
        x = whole.reshape((count * x.shape[0],) + x.shape[1:])
    return x.astype(WIDE)


def reduce_pieces(send, keep):
    near = swap(send, "tensor", 1)
    far = (keep[1].astype(WIDE) + near[1].astype(WIDE)).astype(LOW)
    got = swap(far, "tensor", 2)
    return (keep[0].astype(WIDE) + near[0].astype(WIDE) + got.astype(WIDE)).astype(LOW)


def body(
    hidden_in,
    out_grad,
    teacher,
    valid_mask,
    prefix,
    gain_attn,
    w_qkv,
    w_out,
    gain_mlp,
    w_up,
    b_up,
    w_down,
    b_down,
):
    own, seqs, d = hidden_in.shape
    n_tensor = lax.axis_size("tensor")
    rows = own * n_tensor
    length = teacher.shape[0]
    width = w_qkv.shape[2]
    assert seqs == 1 and n_tensor == 4 and rows == 2 * length
    tile = min(256, own)
    me = lax.axis_index("tensor")
    x = hidden_in.reshape(own, d)
    pieces = gather_pieces(x)

    own_valid = jnp.sum(valid_mask).astype(WIDE)
    count = sum_all(jnp.broadcast_to(own_valid, (8, 128)))[0, 0]
    token_total = length * seqs * lax.axis_size("dp")
    ratio = (token_total / count).reshape(1)
    start = jnp.minimum(me * own, length - own)
    noisy = (me * own < length).astype(WIDE)
    valid = lax.dynamic_slice_in_dim(valid_mask, start, own, 0).astype(WIDE) * noisy
    teach = lax.dynamic_slice_in_dim(teacher.reshape(length, d), start, own, 0)

    w_up_, w_down_, w_out_, b_up_, _ = lax.optimization_barrier(
        (w_up, w_down, w_out, b_up.reshape(1, -1), pieces[2])
    )
    outs = gather_pieces(w_out_)
    ups = gather_pieces(w_up_)
    biases = gather_pieces(b_up_)
    downs = gather_pieces(w_down_)

    half = HEAD_DIM // 2
    freqs = jnp.exp(-jnp.log(10000.0) * jnp.arange(half, dtype=WIDE) * 2.0 / HEAD_DIM)
    angles = jnp.arange(length, dtype=WIDE)[:, None] * freqs[None, :]
    cos = jnp.tile(jnp.cos(angles), (1, width // half))
    sin = jnp.tile(jnp.sin(angles), (1, width // half))
    meta = jnp.stack([prefix[0], me.astype(jnp.int32)])
    w3 = jnp.transpose(w_qkv, (1, 0, 2))
    act_one, q, k, v, mix, lse = attn_forward(
        meta, pieces, gain_attn.reshape(1, d), w3, cos, sin, tile
    )
    mixed = exchange(tuple(mix[b] for b in range(4)))
    (
        layer_out, hid, act_two, gol, gpl, gres, grl, g0, g1, g2, g3, vec,
    ) = mlp(
        ratio, x, mixed, outs, ups, downs, biases, gain_mlp.reshape(1, d),
        b_down.reshape(1, d), teach, valid, out_grad.reshape(own, d),
    )
    grads = exchange((g0, g1, g2, g3))
    down_send, down_keep = down_grad(hid, gol)
    up_send, up_keep = up_grad(act_two, gpl, mixed, grl)
    down_own = reduce_pieces(down_send, down_keep)
    up_own = reduce_pieces(up_send, up_keep)

    g = attn_backward(meta, q, k, v, mix, grads, lse, cos, sin, tile)
    row_send, row_keep = rows_grad(g, w3)
    near = swap(row_send, "tensor", 1)
    far = swap((row_keep[1].astype(WIDE) + near[1].astype(WIDE)).astype(LOW), "tensor", 2)
    qkv_part, gain_part = qkv_grad(act_one, g, w3)
    grad_input = input_grad(x, gain_attn.reshape(1, d), row_keep, near, far, gres)

    down_sum = reduce_over_dp(down_own)
    up_out_sum = reduce_over_dp(up_own)
    qkv_sum = reduce_over_dp(qkv_part.reshape(3 * d, width))

    others = [swap(vec, "tensor", b) for b in range(1, 4)]
    bias_up = vec[0] + others[0][1] + others[1][2] + others[2][3]
    rest = vec[4:7] + others[0][4:7] + others[1][4:7] + others[2][4:7]
    small = sum_all(jnp.concatenate([bias_up[None], rest], 0))
    gain_own = (gain_part[:, 0] / gain_attn).reshape(1, d)
    gain_own = gain_own + sum(swap(gain_own, "tensor", b) for b in range(1, 4))
    gain_attn_sum = sum_all(gain_own)[0]
    distill_loss = small[3, 0] / count
    return (
        layer_out.reshape(own, seqs, d),
        grad_input.reshape(own, seqs, d),
        distill_loss,
        gain_attn_sum,
        jnp.transpose(qkv_sum.reshape(3, d, width), (1, 0, 2)),
        up_out_sum[d:],
        small[2],
        up_out_sum[:d],
        small[0],
        down_sum,
        small[1],
    )


def solution(mesh):
    placed = (
        P("tensor", "dp", None),
        P("tensor", "dp", None),
        P(None, "dp", None),
        P(None, "dp"),
        P("dp"),
        P(),
        P(None, None, "tensor"),
        P("tensor", None),
        P(),
        P(None, "tensor"),
        P("tensor"),
        P("tensor", None),
        P(),
    )
    return jax.shard_map(
        body,
        mesh=mesh,
        in_specs=placed,
        out_specs=(
            P("tensor", "dp", None),
            P("tensor", "dp", None),
            P(),
            P(),
            P(None, None, "tensor"),
            P("tensor", None),
            P(),
            P(None, "tensor"),
            P("tensor"),
            P("tensor", None),
            P(),
        ),
        check_vma=False,
    )
```
